32 devices in a mesh: band: 4 (over y, core), shard: 8 (over z, x).
Axes of the slice: x: 2, y: 2, z: 4, core: 2. Of those that a mesh axis runs over, the one named last changes fastest.
Arguments:
- activations: bfloat16 [512, 2304], P('shard'), may hold values from -6 to 6
- encoder: bfloat16 [2304, 16384], P(None, ('band', 'shard')), may hold values from -0.125 to 0.125
- encoder_bias: float32 [16384], P(('band', 'shard')), may hold values from -1 to -0.25
- decoder: bfloat16 [16384, 2304], P(('band', 'shard')), may hold values from -0.125 to 0.125
Outputs:
- losses: float32 [4], replicated
- encoder_grad: bfloat16 [2304, 16384], P(None, ('band', 'shard'))
- decoder_grad: bfloat16 [16384, 2304], P(('band', 'shard'))
The draws below stay inside these ranges and needn't reach their ends.
All inputs are finite; a program needn't handle non-finite values.
Results may differ from the reference program's by a relative error of at most 0.006.
Values may be sent and summed in bfloat16 or wider, within the bound.
A program may use at most 128 MiB of HBM per device.

```python
import jax
import jax.numpy as jnp
from jax import lax

D = 2304
LATENTS = 16384
ROWS = 512
N_BAND = 4


def block_levels(key, extent, cuts, least, top_value):
    factor_of = 1.0
    for position, shards_of in cuts:
        steps = jax.random.uniform(jax.random.fold_in(jax.random.fold_in(key, 6), position), (shards_of,), jnp.float32, least / len(cuts), top_value / len(cuts))
        factor_of = factor_of * jnp.repeat(jnp.exp(steps), extent[position] // shards_of).reshape((-1,) + (1,) * (len(extent) - 1 - position))
    return factor_of


def bell_draw(key, shape, scale, most, pieces=(), held_as=jnp.bfloat16):
    loudness = block_levels(key, shape, pieces, -0.22, 0.18) if pieces else 1.0
    array = jax.random.normal(key, shape, jnp.float32) * scale * loudness
    return jnp.minimum(jnp.maximum(array, -most), most).astype(held_as)


def setup_inputs(seed: int = 0) -> dict:
    splits = jax.random.split(jax.random.key(seed), 5)
    activations = bell_draw(splits[0], (ROWS, D), 1.0, 6.0, ((0, 8),))
    encoder = bell_draw(splits[1], (D, LATENTS), D ** -0.5, 0.125, ((1, 32),))
    encoder_bias = jnp.clip(-1.0 + 0.75 * jax.random.uniform(splits[2], (LATENTS,), jnp.float32) ** block_levels(splits[2], (LATENTS,), ((0, 32),), -0.2, 0.2), -1.0, -0.25)
    decoder = bell_draw(splits[3], (LATENTS, D), D ** -0.5, 0.125, ((0, 32),))
    return {"activations": activations, "encoder": encoder, "encoder_bias": encoder_bias, "decoder": decoder}


def reference(activations, encoder, encoder_bias, decoder):
    band_count = N_BAND
    width = LATENTS // band_count
    enc_bands = encoder.reshape(D, band_count, width).transpose(1, 0, 2)
    bias_bands = encoder_bias.reshape(band_count, width)
    dec_bands = decoder.reshape(band_count, width, D)

    def forward(items):
        weight, bias, back = items
        preact = jnp.dot(activations, weight, preferred_element_type=jnp.float32) + bias
        linear = jnp.maximum(preact, 0.0)
        active = (linear * linear).astype(jnp.bfloat16)
        part = jnp.dot(active, back, preferred_element_type=jnp.float32)
        return active, linear, part

    active, linears, parts = lax.map(forward, (enc_bands, bias_bands, dec_bands))
    recon = jnp.cumsum(parts, axis=0)
    errors = activations.astype(jnp.float32)[None] - recon
    losses = jnp.sum(errors * errors, axis=(1, 2)) / (ROWS * D)
    suffix = jnp.flip(jnp.cumsum(jnp.flip(errors, 0), axis=0), 0)
    upstream = (-suffix / band_count).astype(jnp.bfloat16)

    def backward(items):
        acted, linear, back, grad = items
        act_grads = jnp.dot(grad, back.T, preferred_element_type=jnp.float32)
        pre_grads = (2.0 * linear * act_grads).astype(jnp.bfloat16)
        enc_grad = jnp.dot(activations.T, pre_grads, preferred_element_type=jnp.float32).astype(jnp.bfloat16)
        dec_grad = jnp.dot(acted.T, grad, preferred_element_type=jnp.float32).astype(jnp.bfloat16)
        return enc_grad, dec_grad

    enc_grads, dec_grads = lax.map(backward, (active, linears, dec_bands, upstream))
    encoder_grad = enc_grads.transpose(1, 0, 2).reshape(D, LATENTS)
    decoder_grad = dec_grads.reshape(LATENTS, D)
    return (losses, encoder_grad, decoder_grad)
```

```python
import functools

import jax
import jax.numpy as jnp
from jax import lax
from jax.experimental import pallas as pl
from jax.experimental.pallas import tpu as pltpu
from jax.sharding import PartitionSpec as P

MESH = pl.DeviceIdType.MESH
PARTS = 4
LAG = 0
SPLIT = 2
F32 = jnp.float32
BF16 = jnp.bfloat16


def factors(count):
    outer = next(a for a in range(1, count + 1) if count % a == 0 and a * a >= count)
    return outer, count // outer


def ring_position(index, outer, inner):
    z, x = index // inner, index % inner
    return x * outer + z + (x % 2) * (outer - 1 - 2 * z)


def ring_index(position, outer, inner):
    x, r = position // outer, position % outer
    z = r + (x % 2) * (outer - 1 - 2 * r)
    return z * inner + x


def tile_of(extent, most):
    return next(t for t in range(most, 0, -128) if extent % t == 0)


def kernel(
    n, nb,
    act_hbm, enc_hbm, bias_ref, dec_hbm,
    gath_t_hbm, ups_hbm, active_hbm, pregr_hbm, loss_ref,
    gath, gath_t, ups, active, pregr,
    enc, dec, linear, part, sendb, recvb, mine_b, mate_b, pair_sum, far, loss_acc, loss1, loss2s, loss2,
    load_sem, own_sem, out_sem,
    ag_s, ag_r, pt_s, pt_r, rs_s, rs_r, bx_s, bx_r, bm_s, bm_r, l1_s, l1_r, l2_s, l2_r, ug_s, ug_r,
):
    width = act_hbm.shape[1]
    rows = act_hbm.shape[0] // PARTS
    half = width // 2
    fwd, bwd = n // 2, n // 2 - 1
    outer, inner = factors(n)
    band = lax.axis_index("band")
    shard = lax.axis_index("shard")
    core, chip, chips = band % 2, band // 2, nb // 2
    sign = 1 - 2 * core
    place = ring_position(shard, outer, inner)
    nxt = {"shard": ring_index((place + n + sign) % n, outer, inner)}
    prv = {"shard": ring_index((place + n - sign) % n, outer, inner)}
    mate = {"band": band + sign}

    load_enc = pltpu.make_async_copy(enc_hbm, enc, load_sem.at[0])
    load_dec = pltpu.make_async_copy(dec_hbm, dec, load_sem.at[1])
    own = [
        pltpu.make_async_copy(
            act_hbm.at[pl.ds(g * SPLIT * rows, SPLIT * rows), :],
            gath.at[pl.ds(g * n * SPLIT * rows, SPLIT * rows), :], own_sem.at[g],
        )
        for g in range(PARTS // SPLIT)
    ]
    for copy in own:
        copy.start()
    load_enc.start()
    load_dec.start()

    barrier = pltpu.get_barrier_semaphore()
    for device in [nxt, prv, {**nxt, **mate}, {**prv, **mate}] + [{"band": (band + i) % nb} for i in range(1, nb)]:
        pl.semaphore_signal(barrier, inc=1, device_id=device, device_id_type=MESH)
    pl.semaphore_wait(barrier, nb + 3)

    started = []
    written = []

    def remote(src, dst, send, recv, device):
        return pltpu.make_async_remote_copy(
            src_ref=src, dst_ref=dst, send_sem=send, recv_sem=recv, device_id=device, device_id_type=MESH
        )

    def go(copy):
        copy.start()
        started.append(copy)
        return copy

    def write(src, dst, index):
        copy = pltpu.make_async_copy(src, dst, out_sem.at[index])
        copy.start()
        written.append(copy)

    tile = tile_of(width, 768)
    step_cols = tile_of(width, 256)
    l2 = []

    def batch(m):
        g, h = m // SPLIT, m % SPLIT
        tall = SPLIT * rows
        base = g * n * tall

        def at(slot):
            return pl.ds(base + slot * tall + h * rows, rows)

        everything = pl.ds(base, n * tall)

        def columns(t):
            return pl.ds(pl.multiple_of((core if t % 2 == 0 else 1 - core) * half, 128), half)

        def held(slot, t):
            return gath.at[pl.ds(base + slot * tall, tall), columns(t)]

        mine = act_hbm.at[pl.ds(g * tall, tall), columns(0)]

        def gather_back(t):
            src = mine if t == 1 else held(t - 1, t - 1)
            return remote(src, held(n - t, t - 1), ag_s.at[g, 0, t], ag_r.at[g, 0, t], {**prv, **mate})

        def gather_ahead(t):
            src = mine if t == 1 else held(n - t + 1, t - 1)
            return remote(src, held(t, t - 1), ag_s.at[g, 1, t], ag_r.at[g, 1, t], {**nxt, **mate})

        def gathered(slot, way, t):
            remote(held(slot, t), held(slot, t), ag_s.at[g, way, t], ag_r.at[g, way, t], mate).wait_recv()

        def mate_copy(slot, t):
            there = n - slot
            return remote(held(slot, t), held(there, t), pt_s.at[g, slot], pt_r.at[g, there], mate)

        def mate_wait(s):
            remote(held(s, 0), held(s, 0), pt_s.at[g, n - s], pt_r.at[g, s], mate).wait_recv()

        def preact():
            span = everything
            value = jnp.dot(gath[span, :], enc[...], preferred_element_type=F32) + bias_ref[...]
            value = jnp.maximum(value, 0.0)
            linear[span, :] = value
            active[span, :] = (value * value).astype(BF16)
            write(active.at[span, :], active_hbm.at[span, :], (0, g))

        def transpose():
            gath_t[:, everything] = gath[everything, :].T
            write(gath_t.at[:, everything], gath_t_hbm.at[:, everything], (1, g))

        def decode():
            span = everything

            def body(i, carry):
                cols = pl.ds(pl.multiple_of(i * tile, tile), tile)
                part[span, cols] = jnp.dot(active[span, :], dec[:, cols], preferred_element_type=F32)
                return carry

            lax.fori_loop(0, width // tile, body, 0)

        if h == 0:
            go(gather_back(1))
            if bwd:
                go(gather_ahead(1))
            own[g].wait()
            yield
            for t in range(1, fwd + 1):
                gathered(n - t, 0, t)
                if t < bwd:
                    go(gather_ahead(t + 1))
                if t <= bwd:
                    gathered(t, 1, t)
                    go(gather_back(t + 1))
                    go(mate_copy(t, t))
                go(mate_copy(n - t, t))
                if t < fwd:
                    yield
            for slot in range(1, n):
                mate_wait(slot)
            if g == 0:
                load_enc.wait()
            preact()
            if g == 0:
                load_dec.wait()
            decode()
        else:
            for _ in range(fwd):
                yield

        rs = {}

        def rs_copy(way, t):
            slot = fwd - t + 1 if way == 0 else fwd + t
            there = slot - 1 if way == 0 else (slot + 1 if slot + 1 < n else fwd)
            return remote(
                sendb.at[m * n + slot], recvb.at[m * n + there], rs_s.at[m, way, t], rs_r.at[m, way, t],
                nxt if way == 0 else prv,
            )

        for t in range(1, fwd + 1):
            for way in (0, 1):
                if way == 1 and t > bwd:
                    continue
                slot = fwd - t + 1 if way == 0 else fwd + t
                value = part[at(slot), :]
                if t > 1:
                    rs[way, t - 1].wait_recv()
                    value = value + recvb[m * n + slot].astype(F32)
                sendb[m * n + slot] = value.astype(BF16)
                rs[way, t] = go(rs_copy(way, t))
            yield
        if bwd:
            rs[1, bwd].wait_recv()
        rs[0, fwd].wait_recv()
        value = part[at(0), :] + recvb[m * n].astype(F32)
        if bwd:
            value = value + recvb[m * n + fwd].astype(F32)
        part[at(0), :] = value
        mine_b[m] = value.astype(BF16)
        go(remote(mine_b.at[m], mate_b.at[m], bm_s.at[m, 0], bm_r.at[m, 0], mate))
        remote(mine_b.at[m], mate_b.at[m], bm_s.at[m, 0], bm_r.at[m, 0], mate).wait_recv()
        share = pl.ds(pl.multiple_of(core * half, 128), half)
        for i in range(1, chips):
            higher = chip + i < chips
            own_weight = jnp.where(higher, 1, nb - band).astype(F32)
            mate_weight = jnp.where(higher, 1, nb - band - sign).astype(F32)
            pair_sum[m, i] = (
                own_weight * mine_b[m, :, share].astype(F32) + mate_weight * mate_b[m, :, share].astype(F32)
            ).astype(BF16)
            go(remote(
                pair_sum.at[m, i], far.at[m, i, :, share], bx_s.at[m, i], bx_r.at[m, i],
                {"band": (band + 2 * i) % nb},
            ))
        yield
        other = pl.ds(pl.multiple_of((1 - core) * half, 128), half)
        for i in range(1, chips):
            remote(pair_sum.at[m, i], far.at[m, i, :, share], bx_s.at[m, i], bx_r.at[m, i], mate).wait_recv()
            go(remote(far.at[m, i, :, share], far.at[m, i, :, share], bm_s.at[m, i], bm_r.at[m, i], mate))
        for i in range(1, chips):
            remote(far.at[m, i, :, other], far.at[m, i, :, other], bm_s.at[m, i], bm_r.at[m, i], mate).wait_recv()

        def errors(i, carry):
            cols = pl.ds(pl.multiple_of(i * step_cols, step_cols), step_cols)
            beside = mate_b[m, :, cols].astype(F32)
            error = gath[at(0), cols].astype(F32) - part[at(0), cols] - core.astype(F32) * beside
            later = ((1 - core) * (nb - band - 1)).astype(F32) * beside
            for k in range(1, chips):
                value = far[m, k, :, cols].astype(F32)
                error = error - jnp.where(chip >= k, 1.0, 0.0) * value
                later = later + jnp.where(chip >= k, 0.0, 1.0) * value
            loss_acc[pl.ds(m, 1), cols] = jnp.sum(error * error, axis=0, keepdims=True)
            ups[at(0), cols] = ((later - (nb - band).astype(F32) * error) / nb).astype(BF16)
            return carry

        lax.fori_loop(0, width // step_cols, errors, 0)

        def ug_copy(way, t):
            if way == 0:
                slot, there, device = (n - t + 1) % n, n - t, nxt
            else:
                slot, there, device = t - 1, t, prv
            return remote(ups.at[at(slot), :], ups.at[at(there), :], ug_s.at[m, way, t], ug_r.at[m, way, t], device)

        def backward():
            span = everything
            grads = lax.dot_general(ups[span, :], dec[...], (((1,), (1,)), ((), ())), preferred_element_type=F32)
            pregr[span, :] = (2.0 * linear[span, :] * grads).astype(BF16)
            write(pregr.at[span, :], pregr_hbm.at[span, :], (3, g))

        ug = {}
        for way in (0, 1):
            if way == 0 or bwd:
                ug[way, 1] = go(ug_copy(way, 1))
        if m == PARTS - 1:
            loss1[band] = jnp.full((8, 128), jnp.sum(loss_acc[...]), F32)
            for i in range(1, nb):
                go(remote(loss1.at[band], loss1.at[band], l1_s.at[i], l1_r.at[i], {"band": (band + i) % nb}))
        yield
        for t in range(1, fwd + 1):
            if m == PARTS - 1 and t == min(2, fwd):
                for i in range(1, nb):
                    other = (band + nb - i) % nb
                    remote(loss1.at[other], loss1.at[other], l1_s.at[i], l1_r.at[i], mate).wait_recv()
                for k in range(nb):
                    loss2s[k:k + 1, :] = loss1[k, 0:1, :]
                for i in range(1, n):
                    l2.append(go(remote(loss2s, loss2.at[i], l2_s.at[i], l2_r.at[i], {"shard": (shard + i) % n})))
            for way in (0, 1):
                last = fwd if way == 0 else bwd
                if t > last:
                    continue
                ug[way, t].wait_recv()
                if t < last:
                    ug[way, t + 1] = go(ug_copy(way, t + 1))
            if t == 1 and h == 0:
                transpose()
            if t < fwd:
                yield
        if h == SPLIT - 1:
            write(ups.at[everything, :], ups_hbm.at[everything, :], (2, g))
            backward()

    work = [batch(m) for m in range(PARTS)]
    done = set()
    turn = 0
    while len(done) < PARTS:
        for m in range(PARTS):
            if m in done or turn < m * LAG:
                continue
            if next(work[m], "end") == "end":
                done.add(m)
        turn += 1
    for copy in l2:
        copy.wait_recv()
    total = loss2s[...]
    for i in range(1, n):
        total = total + loss2[i]
    for k in range(nb):
        loss_ref[k] = jnp.sum(total[k:k + 1, 0:1]) / (n * act_hbm.shape[0] * width)
    for copy in started:
        copy.wait_send()
    for copy in written:
        copy.wait()


def on_device(n, nb, activations, encoder, encoder_bias, decoder):
    local, width = activations.shape
    latents = encoder.shape[1]
    rows = local // PARTS
    every = n * local
    sem = pltpu.SemaphoreType.DMA
    vmem = pl.BlockSpec(memory_space=pltpu.VMEM)
    hbm = pl.BlockSpec(memory_space=pl.ANY)
    steps = n // 2 + 1
    gathered_t, upstream, active, pre_grads, losses = pl.pallas_call(
        functools.partial(kernel, n, nb),
        out_shape=(
            jax.ShapeDtypeStruct((width, every), BF16),
            jax.ShapeDtypeStruct((every, width), BF16),
            jax.ShapeDtypeStruct((every, latents), BF16),
            jax.ShapeDtypeStruct((every, latents), BF16),
            jax.ShapeDtypeStruct((nb,), F32),
        ),
        in_specs=[hbm, hbm, vmem, hbm],
        out_specs=[hbm] * 4 + [pl.BlockSpec(memory_space=pltpu.SMEM)],
        scratch_shapes=[
            pltpu.VMEM((every, width), BF16),
            pltpu.VMEM((width, every), BF16),
            pltpu.VMEM((every, width), BF16),
            pltpu.VMEM((every, latents), BF16),
            pltpu.VMEM((every, latents), BF16),
            pltpu.VMEM((width, latents), BF16),
            pltpu.VMEM((latents, width), BF16),
            pltpu.VMEM((every, latents), F32),
            pltpu.VMEM((every, width), F32),
            pltpu.VMEM((PARTS * n, rows, width), BF16),
            pltpu.VMEM((PARTS * n, rows, width), BF16),
            pltpu.VMEM((PARTS, rows, width), BF16),
            pltpu.VMEM((PARTS, rows, width), BF16),
            pltpu.VMEM((PARTS, nb // 2, rows, width // 2), BF16),
            pltpu.VMEM((PARTS, nb // 2, rows, width), BF16),
            pltpu.VMEM((PARTS, width), F32),
            pltpu.VMEM((nb, 8, 128), F32),
            pltpu.VMEM((nb, 128), F32),
            pltpu.VMEM((n, nb, 128), F32),
            sem((2,)), sem((PARTS,)), sem((4, PARTS)),
            sem((PARTS, 2, steps)), sem((PARTS, 2, steps)),
            sem((PARTS, n)), sem((PARTS, n)),
            sem((PARTS, 2, steps)), sem((PARTS, 2, steps)),
            sem((PARTS, nb)), sem((PARTS, nb)),
            sem((PARTS, nb)), sem((PARTS, nb)),
            sem((nb,)), sem((nb,)),
            sem((n,)), sem((n,)),
            sem((PARTS, 2, steps)), sem((PARTS, 2, steps)),
        ],
        compiler_params=pltpu.CompilerParams(
            collective_id=0, has_side_effects=True, vmem_limit_bytes=60 * 1024 * 1024
        ),
    )(activations, encoder, encoder_bias.reshape(1, latents), decoder)
    def grads(e_ref, f_ref, g_ref, h_ref, eo_ref, do_ref):
        eo_ref[...] = jnp.dot(e_ref[...], f_ref[...], preferred_element_type=F32).astype(BF16)
        do_ref[...] = lax.dot_general(
            g_ref[...], h_ref[...], (((0,), (0,)), ((), ())), preferred_element_type=F32
        ).astype(BF16)

    wide = tile_of(width, 1152)
    encoder_grad, decoder_grad = pl.pallas_call(
        grads,
        grid=(width // wide,),
        out_shape=(
            jax.ShapeDtypeStruct((width, latents), BF16),
            jax.ShapeDtypeStruct((latents, width), BF16),
        ),
        in_specs=[
            pl.BlockSpec((wide, every), lambda i: (i, 0)),
            pl.BlockSpec((every, latents), lambda i: (0, 0)),
            pl.BlockSpec((every, latents), lambda i: (0, 0)),
            pl.BlockSpec((every, wide), lambda i: (0, i)),
        ],
        out_specs=[
            pl.BlockSpec((wide, latents), lambda i: (i, 0)),
            pl.BlockSpec((latents, wide), lambda i: (0, i)),
        ],
        compiler_params=pltpu.CompilerParams(vmem_limit_bytes=60 * 1024 * 1024),
    )(gathered_t, pre_grads, active, upstream)
    return losses, encoder_grad, decoder_grad


def solution(mesh):
    n, nb = mesh.shape["shard"], mesh.shape["band"]
    return jax.shard_map(
        functools.partial(on_device, n, nb),
        mesh=mesh,
        in_specs=(
            P("shard", None),
            P(None, ("band", "shard")),
            P(("band", "shard")),
            P(("band", "shard"), None),
        ),
        out_specs=(P(), P(None, ("band", "shard")), P(("band", "shard"), None)),
        check_vma=False,
    )
```

```python
import functools

import jax
import jax.numpy as jnp
from jax import lax
from jax.experimental import pallas as pl
from jax.experimental.pallas import tpu as pltpu
from jax.sharding import PartitionSpec as P

MESH = pl.DeviceIdType.MESH
PARTS = 4
LAG = 0
SPLIT = 2
F32 = jnp.float32
BF16 = jnp.bfloat16


def factors(count):
    outer = next(a for a in range(1, count + 1) if count % a == 0 and a * a >= count)
    return outer, count // outer


def ring_position(index, outer, inner):
    z, x = index // inner, index % inner
    return x * outer + z + (x % 2) * (outer - 1 - 2 * z)


def ring_index(position, outer, inner):
    x, r = position // outer, position % outer
    z = r + (x % 2) * (outer - 1 - 2 * r)
    return z * inner + x


def tile_of(extent, most):
    return next(t for t in range(most, 0, -128) if extent % t == 0)


def kernel(
    n, nb,
    act_hbm, enc_hbm, bias_ref, dec_hbm,
    gath_t_hbm, ups_hbm, active_hbm, pregr_hbm, loss_ref,
    gath, gath_t, ups, active, pregr,
    enc, dec, linear, part, sendb, recvb, mine_b, mate_b, pair_sum, far, loss_acc, loss1, loss2s, loss2,
    load_sem, own_sem, out_sem,
    ag_s, ag_r, pt_s, pt_r, rs_s, rs_r, bx_s, bx_r, bm_s, bm_r, l1_s, l1_r, l2_s, l2_r, ug_s, ug_r,
):
    width = act_hbm.shape[1]
    rows = act_hbm.shape[0] // PARTS
    half = width // 2
    fwd, bwd = n // 2, n // 2 - 1
    outer, inner = factors(n)
    band = lax.axis_index("band")
    shard = lax.axis_index("shard")
    core, chip, chips = band % 2, band // 2, nb // 2
    sign = 1 - 2 * core
    place = ring_position(shard, outer, inner)
    nxt = {"shard": ring_index((place + n + sign) % n, outer, inner)}
    prv = {"shard": ring_index((place + n - sign) % n, outer, inner)}
    mate = {"band": band + sign}

    load_enc = pltpu.make_async_copy(enc_hbm, enc, load_sem.at[0])
    load_dec = pltpu.make_async_copy(dec_hbm, dec, load_sem.at[1])
    barrier = pltpu.get_barrier_semaphore()
    for device in [nxt, prv, {**nxt, **mate}, {**prv, **mate}] + [{"band": (band + i) % nb} for i in range(1, nb)]:
        pl.semaphore_signal(barrier, inc=1, device_id=device, device_id_type=MESH)
    own = [
        pltpu.make_async_copy(
            act_hbm.at[pl.ds(g * SPLIT * rows, SPLIT * rows), :],
            gath.at[pl.ds(g * n * SPLIT * rows, SPLIT * rows), :], own_sem.at[g],
        )
        for g in range(PARTS // SPLIT)
    ]
    for copy in own:
        copy.start()
    load_enc.start()
    load_dec.start()

    pl.semaphore_wait(barrier, nb + 3)

    started = []
    written = []

    def remote(src, dst, send, recv, device):
        return pltpu.make_async_remote_copy(
            src_ref=src, dst_ref=dst, send_sem=send, recv_sem=recv, device_id=device, device_id_type=MESH
        )

    def go(copy):
        copy.start()
        started.append(copy)
        return copy

    def write(src, dst, index):
        copy = pltpu.make_async_copy(src, dst, out_sem.at[index])
        copy.start()
        written.append(copy)

    tile = tile_of(width, 768)
    step_cols = tile_of(width, 768)
    l2 = []

    def batch(m):
        g, h = m // SPLIT, m % SPLIT
        tall = SPLIT * rows
        base = g * n * tall

        def at(slot):
            return pl.ds(base + slot * tall + h * rows, rows)

        everything = pl.ds(base, n * tall)

        def columns(t):
            return pl.ds(pl.multiple_of((core if t % 2 == 0 else 1 - core) * half, 128), half)

        def held(slot, t):
            return gath.at[pl.ds(base + slot * tall, tall), columns(t)]

        mine = act_hbm.at[pl.ds(g * tall, tall), columns(0)]

        def gather_back(t):
            src = mine if t == 1 else held(t - 1, t - 1)
            return remote(src, held(n - t, t - 1), ag_s.at[g, 0, t], ag_r.at[g, 0, t], {**prv, **mate})

        def gather_ahead(t):
            src = mine if t == 1 else held(n - t + 1, t - 1)
            return remote(src, held(t, t - 1), ag_s.at[g, 1, t], ag_r.at[g, 1, t], {**nxt, **mate})

        def gathered(slot, way, t):
            remote(held(slot, t), held(slot, t), ag_s.at[g, way, t], ag_r.at[g, way, t], mate).wait_recv()

        def mate_copy(slot, t):
            there = n - slot
            return remote(held(slot, t), held(there, t), pt_s.at[g, slot], pt_r.at[g, there], mate)

        def mate_wait(s):
            remote(held(s, 0), held(s, 0), pt_s.at[g, n - s], pt_r.at[g, s], mate).wait_recv()

        def preact():
            span = everything
            value = jnp.dot(gath[span, :], enc[...], preferred_element_type=F32) + bias_ref[...]
            value = jnp.maximum(value, 0.0)
            linear[span, :] = value
            active[span, :] = (value * value).astype(BF16)
            write(active.at[span, :], active_hbm.at[span, :], (0, g))

        def transpose():
            gath_t[:, everything] = gath[everything, :].T
            write(gath_t.at[:, everything], gath_t_hbm.at[:, everything], (1, g))

        def decode():
            span = everything

            def body(i, carry):
                cols = pl.ds(pl.multiple_of(i * tile, tile), tile)
                part[span, cols] = jnp.dot(active[span, :], dec[:, cols], preferred_element_type=F32)
                return carry

            lax.fori_loop(0, width // tile, body, 0)

        if h == 0:
            go(gather_back(1))
            if bwd:
                go(gather_ahead(1))
            own[g].wait()
            yield
            for t in range(1, fwd + 1):
                gathered(n - t, 0, t)
                if t < bwd:
                    go(gather_ahead(t + 1))
                if t <= bwd:
                    gathered(t, 1, t)
                    go(gather_back(t + 1))
                    go(mate_copy(t, t))
                go(mate_copy(n - t, t))
                if t < fwd:
                    yield
            for slot in range(1, n):
                mate_wait(slot)
            if g == 0:
                load_enc.wait()
            preact()
            if g == 0:
                load_dec.wait()
            decode()
        else:
            for _ in range(fwd):
                yield

        rs = {}

        def rs_copy(way, t):
            slot = fwd - t + 1 if way == 0 else fwd + t
            there = slot - 1 if way == 0 else (slot + 1 if slot + 1 < n else fwd)
            return remote(
                sendb.at[m * n + slot], recvb.at[m * n + there], rs_s.at[m, way, t], rs_r.at[m, way, t],
                nxt if way == 0 else prv,
            )

        for t in range(1, fwd + 1):
            for way in (0, 1):
                if way == 1 and t > bwd:
                    continue
                slot = fwd - t + 1 if way == 0 else fwd + t
                value = part[at(slot), :]
                if t > 1:
                    rs[way, t - 1].wait_recv()
                    value = value + recvb[m * n + slot].astype(F32)
                sendb[m * n + slot] = value.astype(BF16)
                rs[way, t] = go(rs_copy(way, t))
            if t == 1 and h == SPLIT - 1:
                transpose()
            yield
        if bwd:
            rs[1, bwd].wait_recv()
        rs[0, fwd].wait_recv()
        value = part[at(0), :] + recvb[m * n].astype(F32)
        if bwd:
            value = value + recvb[m * n + fwd].astype(F32)
        part[at(0), :] = value
        mine_b[m] = value.astype(BF16)
        go(remote(mine_b.at[m], mate_b.at[m], bm_s.at[m, 0], bm_r.at[m, 0], mate))
        remote(mine_b.at[m], mate_b.at[m], bm_s.at[m, 0], bm_r.at[m, 0], mate).wait_recv()
        share = pl.ds(pl.multiple_of(core * half, 128), half)
        for i in range(1, chips):
            higher = chip + i < chips
            own_weight = jnp.where(higher, 1, nb - band).astype(F32)
            mate_weight = jnp.where(higher, 1, nb - band - sign).astype(F32)
            pair_sum[m, i] = (
                own_weight * mine_b[m, :, share].astype(F32) + mate_weight * mate_b[m, :, share].astype(F32)
            ).astype(BF16)
            go(remote(
                pair_sum.at[m, i], far.at[m, i, :, share], bx_s.at[m, i], bx_r.at[m, i],
                {"band": (band + 2 * i) % nb + sign},
            ))
        yield
        other = pl.ds(pl.multiple_of((1 - core) * half, 128), half)
        for i in range(1, chips):
            remote(pair_sum.at[m, i], far.at[m, i, :, other], bx_s.at[m, i], bx_r.at[m, i], mate).wait_recv()
            go(remote(far.at[m, i, :, other], far.at[m, i, :, other], bm_s.at[m, i], bm_r.at[m, i], mate))
        for i in range(1, chips):
            remote(far.at[m, i, :, share], far.at[m, i, :, share], bm_s.at[m, i], bm_r.at[m, i], mate).wait_recv()

        def errors(i, carry):
            cols = pl.ds(pl.multiple_of(i * step_cols, step_cols), step_cols)
            beside = mate_b[m, :, cols].astype(F32)
            error = gath[at(0), cols].astype(F32) - part[at(0), cols] - core.astype(F32) * beside
            later = ((1 - core) * (nb - band - 1)).astype(F32) * beside
            for k in range(1, chips):
                value = far[m, k, :, cols].astype(F32)
                error = error - jnp.where(chip >= k, 1.0, 0.0) * value
                later = later + jnp.where(chip >= k, 0.0, 1.0) * value
            loss_acc[pl.ds(m, 1), cols] = jnp.sum(error * error, axis=0, keepdims=True)
            ups[at(0), cols] = ((later - (nb - band).astype(F32) * error) / nb).astype(BF16)
            return carry

        lax.fori_loop(0, width // step_cols, errors, 0)

        def ug_copy(way, t):
            if way == 0:
                slot, there, device = (n - t + 1) % n, n - t, nxt
            else:
                slot, there, device = t - 1, t, prv
            return remote(ups.at[at(slot), :], ups.at[at(there), :], ug_s.at[m, way, t], ug_r.at[m, way, t], device)

        def backward():
            span = everything
            grads = lax.dot_general(ups[span, :], dec[...], (((1,), (1,)), ((), ())), preferred_element_type=F32)
            pregr[span, :] = (2.0 * linear[span, :] * grads).astype(BF16)
            write(pregr.at[span, :], pregr_hbm.at[span, :], (3, g))

        ug = {}
        for way in (0, 1):
            if way == 0 or bwd:
                ug[way, 1] = go(ug_copy(way, 1))
        if m == PARTS - 1:
            loss1[band] = jnp.full((8, 128), jnp.sum(loss_acc[...]), F32)
            for i in range(1, nb):
                go(remote(loss1.at[band], loss1.at[band], l1_s.at[i], l1_r.at[i], {"band": (band + i) % nb}))
        yield
        for t in range(1, fwd + 1):
            if m == PARTS - 1 and t == min(2, fwd):
                for i in range(1, nb):
                    other = (band + nb - i) % nb
                    remote(loss1.at[other], loss1.at[other], l1_s.at[i], l1_r.at[i], mate).wait_recv()
                for k in range(nb):
                    loss2s[k:k + 1, :] = loss1[k, 0:1, :]
                for i in range(1, n):
                    l2.append(go(remote(loss2s, loss2.at[i], l2_s.at[i], l2_r.at[i], {"shard": (shard + i) % n})))
            for way in (0, 1):
                last = fwd if way == 0 else bwd
                if t > last:
                    continue
                ug[way, t].wait_recv()
                if t < last:
                    ug[way, t + 1] = go(ug_copy(way, t + 1))
            if t < fwd:
                yield
        if h == SPLIT - 1:
            write(ups.at[everything, :], ups_hbm.at[everything, :], (2, g))
            backward()

    work = [batch(m) for m in range(PARTS)]
    done = set()
    turn = 0
    while len(done) < PARTS:
        for m in range(PARTS):
            if m in done or turn < m * LAG:
                continue
            if next(work[m], "end") == "end":
                done.add(m)
        turn += 1
    for copy in l2:
        copy.wait_recv()
    total = loss2s[...]
    for i in range(1, n):
        total = total + loss2[i]
    for k in range(nb):
        loss_ref[k] = jnp.sum(total[k:k + 1, 0:1]) / (n * act_hbm.shape[0] * width)
    for copy in started:
        copy.wait_send()
    for copy in written:
        copy.wait()


def on_device(n, nb, activations, encoder, encoder_bias, decoder):
    local, width = activations.shape
    latents = encoder.shape[1]
    rows = local // PARTS
    every = n * local
    sem = pltpu.SemaphoreType.DMA
    vmem = pl.BlockSpec(memory_space=pltpu.VMEM)
    hbm = pl.BlockSpec(memory_space=pl.ANY)
    steps = n // 2 + 1
    gathered_t, upstream, active, pre_grads, losses = pl.pallas_call(
        functools.partial(kernel, n, nb),
        out_shape=(
            jax.ShapeDtypeStruct((width, every), BF16),
            jax.ShapeDtypeStruct((every, width), BF16),
            jax.ShapeDtypeStruct((every, latents), BF16),
            jax.ShapeDtypeStruct((every, latents), BF16),
            jax.ShapeDtypeStruct((nb,), F32),
        ),
        in_specs=[hbm, hbm, vmem, hbm],
        out_specs=[hbm] * 4 + [pl.BlockSpec(memory_space=pltpu.SMEM)],
        scratch_shapes=[
            pltpu.VMEM((every, width), BF16),
            pltpu.VMEM((width, every), BF16),
            pltpu.VMEM((every, width), BF16),
            pltpu.VMEM((every, latents), BF16),
            pltpu.VMEM((every, latents), BF16),
            pltpu.VMEM((width, latents), BF16),
            pltpu.VMEM((latents, width), BF16),
            pltpu.VMEM((every, latents), F32),
            pltpu.VMEM((every, width), F32),
            pltpu.VMEM((PARTS * n, rows, width), BF16),
            pltpu.VMEM((PARTS * n, rows, width), BF16),
            pltpu.VMEM((PARTS, rows, width), BF16),
            pltpu.VMEM((PARTS, rows, width), BF16),
            pltpu.VMEM((PARTS, nb // 2, rows, width // 2), BF16),
            pltpu.VMEM((PARTS, nb // 2, rows, width), BF16),
            pltpu.VMEM((PARTS, width), F32),
            pltpu.VMEM((nb, 8, 128), F32),
            pltpu.VMEM((nb, 128), F32),
            pltpu.VMEM((n, nb, 128), F32),
            sem((2,)), sem((PARTS,)), sem((4, PARTS)),
            sem((PARTS, 2, steps)), sem((PARTS, 2, steps)),
            sem((PARTS, n)), sem((PARTS, n)),
            sem((PARTS, 2, steps)), sem((PARTS, 2, steps)),
            sem((PARTS, nb)), sem((PARTS, nb)),
            sem((PARTS, nb)), sem((PARTS, nb)),
            sem((nb,)), sem((nb,)),
            sem((n,)), sem((n,)),
            sem((PARTS, 2, steps)), sem((PARTS, 2, steps)),
        ],
        compiler_params=pltpu.CompilerParams(
            collective_id=0, has_side_effects=True, vmem_limit_bytes=60 * 1024 * 1024
        ),
    )(activations, encoder, encoder_bias.reshape(1, latents), decoder)
    def grads(l_hbm, e_ref, f_ref, g_ref, h_ref, lo_hbm, eo_ref, do_ref, l_sem):
        copy = pltpu.make_async_copy(l_hbm, lo_hbm, l_sem.at[0])
        pl.when(pl.program_id(0) == 0)(copy.start)
        pl.when(pl.program_id(0) == pl.num_programs(0) - 1)(copy.wait)
        eo_ref[...] = jnp.dot(e_ref[...], f_ref[...], preferred_element_type=F32).astype(BF16)
        do_ref[...] = lax.dot_general(
            g_ref[...], h_ref[...], (((0,), (0,)), ((), ())), preferred_element_type=F32
        ).astype(BF16)

    wide = tile_of(width, 1152)
    losses, encoder_grad, decoder_grad = pl.pallas_call(
        grads,
        grid=(width // wide,),
        out_shape=(
            jax.ShapeDtypeStruct((nb,), F32),
            jax.ShapeDtypeStruct((width, latents), BF16),
            jax.ShapeDtypeStruct((latents, width), BF16),
        ),
        in_specs=[
            hbm,
            pl.BlockSpec((wide, every), lambda i: (i, 0)),
            pl.BlockSpec((every, latents), lambda i: (0, 0)),
            pl.BlockSpec((every, latents), lambda i: (0, 0)),
            pl.BlockSpec((every, wide), lambda i: (0, i)),
        ],
        out_specs=[
            hbm,
            pl.BlockSpec((wide, latents), lambda i: (i, 0)),
            pl.BlockSpec((latents, wide), lambda i: (0, i)),
        ],
        scratch_shapes=[sem((1,))],
        compiler_params=pltpu.CompilerParams(vmem_limit_bytes=60 * 1024 * 1024),
    )(losses, gathered_t, pre_grads, active, upstream)
    return losses, encoder_grad, decoder_grad


def solution(mesh):
    n, nb = mesh.shape["shard"], mesh.shape["band"]
    return jax.shard_map(
        functools.partial(on_device, n, nb),
        mesh=mesh,
        in_specs=(
            P("shard", None),
            P(None, ("band", "shard")),
            P(("band", "shard")),
            P(("band", "shard"), None),
        ),
        out_specs=(P(), P(None, ("band", "shard")), P(("band", "shard"), None)),
        check_vma=False,
    )
```

```python
import functools

import jax
import jax.numpy as jnp
from jax import lax
from jax.experimental import pallas as pl
from jax.experimental.pallas import tpu as pltpu
from jax.sharding import PartitionSpec as P

MESH = pl.DeviceIdType.MESH
PARTS = 4
LAG = 0
SPLIT = 2
F32 = jnp.float32
BF16 = jnp.bfloat16


def factors(count):
    outer = next(a for a in range(1, count + 1) if count % a == 0 and a * a >= count)
    return outer, count // outer


def ring_position(index, outer, inner):
    z, x = index // inner, index % inner
    return x * outer + z + (x % 2) * (outer - 1 - 2 * z)


def ring_index(position, outer, inner):
    x, r = position // outer, position % outer
    z = r + (x % 2) * (outer - 1 - 2 * r)
    return z * inner + x


def tile_of(extent, most):
    return next(t for t in range(most, 0, -128) if extent % t == 0)


def kernel(
    n, nb,
    act_hbm, enc_hbm, bias_ref, dec_hbm,
    gath_t_hbm, ups_hbm, active_hbm, pregr_hbm, loss_ref,
    gath, gath_t, ups, active, pregr,
    enc, dec, linear, part, sendb, recvb, mine_b, mate_b, pair_sum, far, loss_acc, loss1, loss2s, loss2,
    load_sem, own_sem, out_sem,
    ag_s, ag_r, pt_s, pt_r, rs_s, rs_r, bx_s, bx_r, bm_s, bm_r, l1_s, l1_r, l2_s, l2_r, ug_s, ug_r,
):
    width = act_hbm.shape[1]
    rows = act_hbm.shape[0] // PARTS
    half = width // 2
    fwd, bwd = n // 2, n // 2 - 1
    outer, inner = factors(n)
    band = lax.axis_index("band")
    shard = lax.axis_index("shard")
    core, chip, chips = band % 2, band // 2, nb // 2
    sign = 1 - 2 * core
    place = ring_position(shard, outer, inner)
    nxt = {"shard": ring_index((place + n + sign) % n, outer, inner)}
    prv = {"shard": ring_index((place + n - sign) % n, outer, inner)}
    mate = {"band": band + sign}

    load_enc = pltpu.make_async_copy(enc_hbm, enc, load_sem.at[0])
    load_dec = pltpu.make_async_copy(dec_hbm, dec, load_sem.at[1])
    barrier = pltpu.get_barrier_semaphore()
    for device in [nxt, prv, {**nxt, **mate}, {**prv, **mate}] + [{"band": (band + i) % nb} for i in range(1, nb)]:
        pl.semaphore_signal(barrier, inc=1, device_id=device, device_id_type=MESH)
    own = [
        pltpu.make_async_copy(
            act_hbm.at[pl.ds(g * SPLIT * rows, SPLIT * rows), :],
            gath.at[pl.ds(g * n * SPLIT * rows, SPLIT * rows), :], own_sem.at[g],
        )
        for g in range(PARTS // SPLIT)
    ]
    for copy in own:
        copy.start()
    load_enc.start()
    load_dec.start()

    pl.semaphore_wait(barrier, nb + 3)

    started = []
    written = []

    def remote(src, dst, send, recv, device):
        return pltpu.make_async_remote_copy(
            src_ref=src, dst_ref=dst, send_sem=send, recv_sem=recv, device_id=device, device_id_type=MESH
        )

    def go(copy):
        copy.start()
        started.append(copy)
        return copy

    def write(src, dst, index):
        copy = pltpu.make_async_copy(src, dst, out_sem.at[index])
        copy.start()
        written.append(copy)

    tile = tile_of(width, 768)
    step_cols = tile_of(width, 768)
    l2 = []

    def batch(m):
        g, h = m // SPLIT, m % SPLIT
        tall = SPLIT * rows
        base = g * n * tall

        def at(slot):
            return pl.ds(base + slot * tall + h * rows, rows)

        everything = pl.ds(base, n * tall)
        halves = pl.ds(base, fwd * tall), pl.ds(base + fwd * tall, fwd * tall)

        def columns(t):
            return pl.ds(pl.multiple_of((core if t % 2 == 0 else 1 - core) * half, 128), half)

        def held(slot, t):
            return gath.at[pl.ds(base + slot * tall, tall), columns(t)]

        mine = act_hbm.at[pl.ds(g * tall, tall), columns(0)]

        def gather_back(t):
            src = mine if t == 1 else held(t - 1, t - 1)
            return remote(src, held(n - t, t - 1), ag_s.at[g, 0, t], ag_r.at[g, 0, t], {**prv, **mate})

        def gather_ahead(t):
            src = mine if t == 1 else held(n - t + 1, t - 1)
            return remote(src, held(t, t - 1), ag_s.at[g, 1, t], ag_r.at[g, 1, t], {**nxt, **mate})

        def gathered(slot, way, t):
            remote(held(slot, t), held(slot, t), ag_s.at[g, way, t], ag_r.at[g, way, t], mate).wait_recv()

        def mate_copy(slot, t):
            there = n - slot
            return remote(held(slot, t), held(there, t), pt_s.at[g, slot], pt_r.at[g, there], mate)

        def mate_wait(s):
            remote(held(s, 0), held(s, 0), pt_s.at[g, n - s], pt_r.at[g, s], mate).wait_recv()

        def preact(upper):
            span = halves[upper]
            value = jnp.dot(gath[span, :], enc[...], preferred_element_type=F32) + bias_ref[...]
            value = jnp.maximum(value, 0.0)
            linear[span, :] = value
            active[span, :] = (value * value).astype(BF16)
            write(active.at[span, :], active_hbm.at[span, :], (0, upper * (PARTS // SPLIT) + g))

        def transpose():
            gath_t[:, everything] = gath[everything, :].T
            write(gath_t.at[:, everything], gath_t_hbm.at[:, everything], (1, g))

        def decode(upper):
            span = halves[upper]

            def body(i, carry):
                cols = pl.ds(pl.multiple_of(i * tile, tile), tile)
                part[span, cols] = jnp.dot(active[span, :], dec[:, cols], preferred_element_type=F32)
                return carry

            lax.fori_loop(0, width // tile, body, 0)

        if h == 0:
            go(gather_back(1))
            if bwd:
                go(gather_ahead(1))
            own[g].wait()
            yield
            for t in range(1, fwd + 1):
                if t == fwd:
                    for slot in range(1, fwd):
                        mate_wait(slot)
                    if g == 0:
                        load_enc.wait()
                    preact(0)
                gathered(n - t, 0, t)
                if t < bwd:
                    go(gather_ahead(t + 1))
                if t <= bwd:
                    gathered(t, 1, t)
                    go(gather_back(t + 1))
                    go(mate_copy(t, t))
                go(mate_copy(n - t, t))
                if t < fwd:
                    yield
            for slot in range(fwd, n):
                mate_wait(slot)
            preact(1)
            if g == 0:
                load_dec.wait()
            decode(1)
        else:
            for _ in range(fwd):
                yield

        rs = {}

        def rs_copy(way, t):
            slot = fwd - t + 1 if way == 0 else fwd + t
            there = slot - 1 if way == 0 else (slot + 1 if slot + 1 < n else fwd)
            return remote(
                sendb.at[m * n + slot], recvb.at[m * n + there], rs_s.at[m, way, t], rs_r.at[m, way, t],
                nxt if way == 0 else prv,
            )

        for t in range(1, fwd + 1):
            for way in (0, 1):
                if way == 1 and t > bwd:
                    continue
                slot = fwd - t + 1 if way == 0 else fwd + t
                value = part[at(slot), :]
                if t > 1:
                    rs[way, t - 1].wait_recv()
                    value = value + recvb[m * n + slot].astype(F32)
                sendb[m * n + slot] = value.astype(BF16)
                rs[way, t] = go(rs_copy(way, t))
            yield
            if t == 1 and h == 0:
                decode(0)
            if t == 2 and h == SPLIT - 1:
                transpose()
        if bwd:
            rs[1, bwd].wait_recv()
        rs[0, fwd].wait_recv()
        value = part[at(0), :] + recvb[m * n].astype(F32)
        if bwd:
            value = value + recvb[m * n + fwd].astype(F32)
        part[at(0), :] = value
        mine_b[m] = value.astype(BF16)
        go(remote(mine_b.at[m], mate_b.at[m], bm_s.at[m, 0], bm_r.at[m, 0], mate))
        remote(mine_b.at[m], mate_b.at[m], bm_s.at[m, 0], bm_r.at[m, 0], mate).wait_recv()
        share = pl.ds(pl.multiple_of(core * half, 128), half)
        for i in range(1, chips):
            higher = chip + i < chips
            own_weight = jnp.where(higher, 1, nb - band).astype(F32)
            mate_weight = jnp.where(higher, 1, nb - band - sign).astype(F32)
            pair_sum[m, i] = (
                own_weight * mine_b[m, :, share].astype(F32) + mate_weight * mate_b[m, :, share].astype(F32)
            ).astype(BF16)
            go(remote(
                pair_sum.at[m, i], far.at[m, i, :, share], bx_s.at[m, i], bx_r.at[m, i],
                {"band": (band + 2 * i) % nb + sign},
            ))
        yield
        other = pl.ds(pl.multiple_of((1 - core) * half, 128), half)
        for i in range(1, chips):
            remote(pair_sum.at[m, i], far.at[m, i, :, other], bx_s.at[m, i], bx_r.at[m, i], mate).wait_recv()
            go(remote(far.at[m, i, :, other], far.at[m, i, :, other], bm_s.at[m, i], bm_r.at[m, i], mate))
        for i in range(1, chips):
            remote(far.at[m, i, :, share], far.at[m, i, :, share], bm_s.at[m, i], bm_r.at[m, i], mate).wait_recv()

        def errors(i, carry):
            cols = pl.ds(pl.multiple_of(i * step_cols, step_cols), step_cols)
            beside = mate_b[m, :, cols].astype(F32)
            error = gath[at(0), cols].astype(F32) - part[at(0), cols] - core.astype(F32) * beside
            later = ((1 - core) * (nb - band - 1)).astype(F32) * beside
            for k in range(1, chips):
                value = far[m, k, :, cols].astype(F32)
                error = error - jnp.where(chip >= k, 1.0, 0.0) * value
                later = later + jnp.where(chip >= k, 0.0, 1.0) * value
            loss_acc[pl.ds(m, 1), cols] = jnp.sum(error * error, axis=0, keepdims=True)
            ups[at(0), cols] = ((later - (nb - band).astype(F32) * error) / nb).astype(BF16)
            return carry

        lax.fori_loop(0, width // step_cols, errors, 0)

        def ug_copy(way, t):
            if way == 0:
                slot, there, device = (n - t + 1) % n, n - t, nxt
            else:
                slot, there, device = t - 1, t, prv
            return remote(ups.at[at(slot), :], ups.at[at(there), :], ug_s.at[m, way, t], ug_r.at[m, way, t], device)

        def backward():
            span = everything
            grads = lax.dot_general(ups[span, :], dec[...], (((1,), (1,)), ((), ())), preferred_element_type=F32)
            pregr[span, :] = (2.0 * linear[span, :] * grads).astype(BF16)
            write(pregr.at[span, :], pregr_hbm.at[span, :], (3, g))

        ug = {}
        for way in (0, 1):
            if way == 0 or bwd:
                ug[way, 1] = go(ug_copy(way, 1))
        if m == PARTS - 1:
            loss1[band] = jnp.full((8, 128), jnp.sum(loss_acc[...]), F32)
            for i in range(1, nb):
                go(remote(loss1.at[band], loss1.at[band], l1_s.at[i], l1_r.at[i], {"band": (band + i) % nb}))
        yield
        for t in range(1, fwd + 1):
            if m == PARTS - 1 and t == min(2, fwd):
                for i in range(1, nb):
                    other = (band + nb - i) % nb
                    remote(loss1.at[other], loss1.at[other], l1_s.at[i], l1_r.at[i], mate).wait_recv()
                for k in range(nb):
                    loss2s[k:k + 1, :] = loss1[k, 0:1, :]
                for i in range(1, n):
                    l2.append(go(remote(loss2s, loss2.at[i], l2_s.at[i], l2_r.at[i], {"shard": (shard + i) % n})))
            for way in (0, 1):
                last = fwd if way == 0 else bwd
                if t > last:
                    continue
                ug[way, t].wait_recv()
                if t < last:
                    ug[way, t + 1] = go(ug_copy(way, t + 1))
            if t < fwd:
                yield
        if h == SPLIT - 1:
            write(ups.at[everything, :], ups_hbm.at[everything, :], (2, g))
            backward()

    work = [batch(m) for m in range(PARTS)]
    done = set()
    turn = 0
    while len(done) < PARTS:
        for m in range(PARTS):
            if m in done or turn < m * LAG:
                continue
            if next(work[m], "end") == "end":
                done.add(m)
        turn += 1
    for copy in l2:
        copy.wait_recv()
    total = loss2s[...]
    for i in range(1, n):
        total = total + loss2[i]
    for k in range(nb):
        loss_ref[k] = jnp.sum(total[k:k + 1, 0:1]) / (n * act_hbm.shape[0] * width)
    for copy in started:
        copy.wait_send()
    for copy in written:
        copy.wait()


def on_device(n, nb, activations, encoder, encoder_bias, decoder):
    local, width = activations.shape
    latents = encoder.shape[1]
    rows = local // PARTS
    every = n * local
    sem = pltpu.SemaphoreType.DMA
    vmem = pl.BlockSpec(memory_space=pltpu.VMEM)
    hbm = pl.BlockSpec(memory_space=pl.ANY)
    steps = n // 2 + 1
    gathered_t, upstream, active, pre_grads, losses = pl.pallas_call(
        functools.partial(kernel, n, nb),
        out_shape=(
            jax.ShapeDtypeStruct((width, every), BF16),
            jax.ShapeDtypeStruct((every, width), BF16),
            jax.ShapeDtypeStruct((every, latents), BF16),
            jax.ShapeDtypeStruct((every, latents), BF16),
            jax.ShapeDtypeStruct((nb,), F32),
        ),
        in_specs=[hbm, hbm, vmem, hbm],
        out_specs=[hbm] * 4 + [pl.BlockSpec(memory_space=pltpu.SMEM)],
        scratch_shapes=[
            pltpu.VMEM((every, width), BF16),
            pltpu.VMEM((width, every), BF16),
            pltpu.VMEM((every, width), BF16),
            pltpu.VMEM((every, latents), BF16),
            pltpu.VMEM((every, latents), BF16),
            pltpu.VMEM((width, latents), BF16),
            pltpu.VMEM((latents, width), BF16),
            pltpu.VMEM((every, latents), F32),
            pltpu.VMEM((every, width), F32),
            pltpu.VMEM((PARTS * n, rows, width), BF16),
            pltpu.VMEM((PARTS * n, rows, width), BF16),
            pltpu.VMEM((PARTS, rows, width), BF16),
            pltpu.VMEM((PARTS, rows, width), BF16),
            pltpu.VMEM((PARTS, nb // 2, rows, width // 2), BF16),
            pltpu.VMEM((PARTS, nb // 2, rows, width), BF16),
            pltpu.VMEM((PARTS, width), F32),
            pltpu.VMEM((nb, 8, 128), F32),
            pltpu.VMEM((nb, 128), F32),
            pltpu.VMEM((n, nb, 128), F32),
            sem((2,)), sem((PARTS,)), sem((4, PARTS)),
            sem((PARTS, 2, steps)), sem((PARTS, 2, steps)),
            sem((PARTS, n)), sem((PARTS, n)),
            sem((PARTS, 2, steps)), sem((PARTS, 2, steps)),
            sem((PARTS, nb)), sem((PARTS, nb)),
            sem((PARTS, nb)), sem((PARTS, nb)),
            sem((nb,)), sem((nb,)),
            sem((n,)), sem((n,)),
            sem((PARTS, 2, steps)), sem((PARTS, 2, steps)),
        ],
        compiler_params=pltpu.CompilerParams(
            collective_id=0, has_side_effects=True, vmem_limit_bytes=60 * 1024 * 1024
        ),
    )(activations, encoder, encoder_bias.reshape(1, latents), decoder)
    def grads(l_hbm, e_ref, f_ref, g_ref, h_ref, lo_hbm, eo_ref, do_ref, l_sem):
        copy = pltpu.make_async_copy(l_hbm, lo_hbm, l_sem.at[0])
        pl.when(pl.program_id(0) == 0)(copy.start)
        pl.when(pl.program_id(0) == pl.num_programs(0) - 1)(copy.wait)
        eo_ref[...] = jnp.dot(e_ref[...], f_ref[...], preferred_element_type=F32).astype(BF16)
        do_ref[...] = lax.dot_general(
            g_ref[...], h_ref[...], (((0,), (0,)), ((), ())), preferred_element_type=F32
        ).astype(BF16)

    wide = tile_of(width, 1152)
    losses, encoder_grad, decoder_grad = pl.pallas_call(
        grads,
        grid=(width // wide,),
        out_shape=(
            jax.ShapeDtypeStruct((nb,), F32),
            jax.ShapeDtypeStruct((width, latents), BF16),
            jax.ShapeDtypeStruct((latents, width), BF16),
        ),
        in_specs=[
            hbm,
            pl.BlockSpec((wide, every), lambda i: (i, 0)),
            pl.BlockSpec((every, latents), lambda i: (0, 0)),
            pl.BlockSpec((every, latents), lambda i: (0, 0)),
            pl.BlockSpec((every, wide), lambda i: (0, i)),
        ],
        out_specs=[
            hbm,
            pl.BlockSpec((wide, latents), lambda i: (i, 0)),
            pl.BlockSpec((latents, wide), lambda i: (0, i)),
        ],
        scratch_shapes=[sem((1,))],
        compiler_params=pltpu.CompilerParams(vmem_limit_bytes=60 * 1024 * 1024),
    )(losses, gathered_t, pre_grads, active, upstream)
    return losses, encoder_grad, decoder_grad


def solution(mesh):
    n, nb = mesh.shape["shard"], mesh.shape["band"]
    return jax.shard_map(
        functools.partial(on_device, n, nb),
        mesh=mesh,
        in_specs=(
            P("shard", None),
            P(None, ("band", "shard")),
            P(("band", "shard")),
            P(("band", "shard"), None),
        ),
        out_specs=(P(), P(None, ("band", "shard")), P(("band", "shard"), None)),
        check_vma=False,
    )
```
